256 devices in a mesh: segment: 8 (over z_lo, core), dp: 32 (over x, y, z_hi).
Axes of the slice: x: 4, y: 4, z: 8 (z_hi: 2, z_lo: 4; z = z_hi * 4 + z_lo), core: 2. Of those that a mesh axis runs over, the one named last changes fastest.
Arguments:
- layer_inputs: bfloat16 [8, 8192, 6144], P('segment', 'dp'), may hold values from -6 to 6
- resid_grad: bfloat16 [8, 8192, 6144], P('segment', 'dp'), may hold values from -3 to 3
- key_grad: bfloat16 [8, 8192, 512], P('segment', 'dp'), may hold values from -4 to 4
- key_weight: bfloat16 [8, 6144, 512], P('segment', 'dp'), may hold values from -0.125 to 0.125
- fim_bounds: int32 [8, 2], P('segment'), may hold values from 1 to 4095
- slot_block: int32 [8, 32], P('segment'), may hold values from 0 to 31, each once within a row
- inv_input: float32 [8, 32, 192, 192], P('segment', 'dp'), may hold values from -1.5 to 10.8, as said below
- inv_head: float32 [8, 4, 128, 128], P('segment'), may hold values from -1.5 to 10.8, as said below
Outputs:
- passed: bfloat16 [8, 8192, 6144], P('segment', 'dp')
- precond: float32 [8, 32, 192, 512], P('segment', 'dp')
- input_grams: float32 [8, 32, 192, 192], P('segment', 'dp')
- head_grams: float32 [8, 4, 128, 128], P('segment')
The draws below stay inside these ranges and needn't reach their ends.
Inputs may be any that keep to these rules, and one draw needn't show every extreme that they name: `slot_block`: each section's row names every block once. `inv_input`: symmetric. `inv_head`: symmetric.
All inputs are finite; a program needn't handle non-finite values.
Results may differ from the reference program's by a relative error of at most 0.0039.
Values may be sent and summed in bfloat16 or wider, within the bound.
No kernel may reach another device: no remote copies, remote signals or barrier semaphores. Data moves between devices by JAX's collectives and lax.ppermute only.
A program may use at most 128 MiB of HBM per device.

```python
import jax
import jax.numpy as jnp
from jax import lax

D = 6144
HD = 128
KVH = 4
KO = 512
BLK = 192
NBLK = 32
TOKENS = 8192
SECTIONS = 8


def dominant_stack(key, leading, order, cubed):
    first_key, second_key = jax.random.split(key)
    uniform_part = jax.random.uniform(first_key, leading + (order, order), jnp.float32, -1.0, 1.0)
    if cubed:
        uniform_part = uniform_part * uniform_part * uniform_part
    symmetric = 0.5 * (uniform_part + jnp.swapaxes(uniform_part, -1, -2))
    off_scale = 6.0 / order
    diagonal = 6.0 * jax.random.uniform(second_key, leading + (order,), jnp.float32, 1.05, 1.8)
    identity = jnp.eye(order, dtype=jnp.float32)
    return symmetric * off_scale * (1.0 - identity) + identity * diagonal[..., None]


def draw_inv_input(key, part):
    return dominant_stack(jax.random.fold_in(key, 11), (SECTIONS, NBLK), BLK, False)


def draw_inv_head(key, part):
    return dominant_stack(jax.random.fold_in(key, 23), (SECTIONS, KVH), HD, False)


def touch_ends(array, own_key, least, high):
    longest = array.shape.index(max(array.shape))
    spots = []
    for shift in (0, 1):
        where = [jax.random.randint(jax.random.fold_in(own_key, axis), (), 0, length) for axis, length in enumerate(array.shape)]
        where[longest] = (where[longest] + shift) % array.shape[longest]
        spots.append(tuple(where))
    return array.at[spots[0]].set(least).at[spots[1]].set(high)


def raised(entries, rng, source, target, blocks, factor):
    owner, partner = [(jnp.arange(entries.shape[axis_at]) // (entries.shape[axis_at] // blocks)).reshape([-1 if axis == axis_at else 1 for axis in range(entries.ndim)]) for axis_at in (source, target)]
    chosen = jax.random.permutation(rng, blocks)[partner]
    strong = (owner == chosen) | (owner == (partner + blocks // 2) % blocks)
    return jnp.where(strong, factor * entries, entries)


def steps_of(rng, dims, shards, low, largest):
    gain, own = 1.0, jax.random.fold_in(rng, 6)
    for axis_at, blocks in shards:
        steps = jnp.exp(jax.random.uniform(jax.random.fold_in(own, axis_at), (blocks,), jnp.float32, low / len(shards), largest / len(shards)))
        gain = gain * jnp.repeat(steps, dims[axis_at] // blocks).reshape([-1 if axis == axis_at else 1 for axis in range(len(dims))])
    return gain


def bell_draw(own_key, dims, width, most, cuts=(), kind=jnp.bfloat16):
    level = steps_of(own_key, dims, cuts, -0.22, 0.18) if cuts else 1.0
    array = jax.random.normal(own_key, dims, jnp.float32) * width * level
    return jnp.minimum(jnp.maximum(array, -most), most).astype(kind)


def gaussian_with(own_key, dims, spread, most, cuts, heavy, kind=jnp.bfloat16):
    entries = spread * jax.random.normal(own_key, dims, jnp.float32)
    if cuts:
        entries = entries * steps_of(own_key, dims, cuts, -0.22, 0.18)
    return jnp.clip(raised(entries, jax.random.fold_in(own_key, 3), *heavy), -most, most).astype(kind)


def setup_inputs(seed: int = 0) -> dict:
    splits = jax.random.split(jax.random.key(seed), 9)
    return {
        "layer_inputs": gaussian_with(splits[0], (SECTIONS, TOKENS, D), 1.0, 6.0, ((0, 8), (1, 32)), (1, 2, 32, 2.75)),
        "resid_grad": bell_draw(splits[1], (SECTIONS, TOKENS, D), 0.5, 3.0, ((0, 8), (1, 32))),
        "key_grad": bell_draw(splits[2], (SECTIONS, TOKENS, KO), 1.0, 4.0, ((0, 8), (1, 32))),
        "key_weight": bell_draw(splits[3], (SECTIONS, D, KO), (4 * KO) ** -0.5, 0.125, ((0, 8), (1, 32))),
        "fim_bounds": touch_ends(jax.random.randint(splits[4], (SECTIONS, 2), 1, TOKENS // 2), jax.random.fold_in(splits[4], 1), 1, (TOKENS // 2) - 1).astype(jnp.int32),
        "slot_block": jax.vmap(lambda own: jax.random.permutation(own, NBLK))(jax.random.split(splits[5], SECTIONS)).reshape((SECTIONS, NBLK)).astype(jnp.int32),
        "inv_input": draw_inv_input(jax.random.fold_in(splits[8], 71), 0),
        "inv_head": draw_inv_head(jax.random.fold_in(splits[8], 71), 0),
    }


rope_base = 100000.0


def fim_positions(bounds):
    token_index = jnp.arange(TOKENS, dtype=jnp.int32)
    prefix_len = bounds[0]
    suffix_len = bounds[1]
    middle_len = TOKENS - prefix_len - suffix_len
    return jnp.where(token_index < prefix_len, token_index, jnp.where(token_index < prefix_len + suffix_len, token_index + middle_len, token_index - suffix_len))


def rope_back(grad_rot, token_pos):
    half_dim = HD // 2
    frequency = jnp.power(jnp.float32(rope_base), -2.0 * jnp.arange(half_dim, dtype=jnp.float32) / HD)
    angle = token_pos.astype(jnp.float32)[:, None] * frequency[None, :]
    cosines = jnp.cos(angle)[:, None, :]
    sine_part = jnp.sin(angle)[:, None, :]
    heads = grad_rot.astype(jnp.float32).reshape(grad_rot.shape[0], KVH, HD)
    first_half = heads[..., :half_dim]
    second_half = heads[..., half_dim:]
    joined = jnp.concatenate([first_half * cosines + second_half * sine_part, second_half * cosines - first_half * sine_part], axis=-1)
    return joined.reshape(grad_rot.shape[0], KVH * HD)


def reference(layer_inputs, resid_grad, key_grad, key_weight, fim_bounds, slot_block, inv_input, inv_head):
    sent_list = []
    precond_list = []
    input_list = []
    head_list = []
    for section in range(SECTIONS):
        inputs_now = layer_inputs[section]
        key_pre = rope_back(key_grad[section], fim_positions(fim_bounds[section])).astype(jnp.bfloat16)
        branch = jnp.dot(key_pre, key_weight[section].T, preferred_element_type=jnp.float32)
        sent_list.append((resid_grad[section].astype(jnp.float32) + branch).astype(jnp.bfloat16))
        weight_grad = jnp.dot(inputs_now.T, key_pre, preferred_element_type=jnp.float32) / TOKENS
        slot_ids = slot_block[section]
        grad_blocks = weight_grad.reshape(NBLK, BLK, KVH * HD)[slot_ids]
        blocked = inputs_now.astype(jnp.float32).reshape(TOKENS, NBLK, BLK)
        grams = jnp.einsum("tcb,tce->cbe", blocked, blocked) / TOKENS
        input_list.append(grams[slot_ids])
        key_heads = key_pre.astype(jnp.float32).reshape(TOKENS, KVH, HD)
        head_list.append(jnp.einsum("thd,the->hde", key_heads, key_heads) / TOKENS)
        left_side = jnp.einsum("cab,cbk->cak", inv_input[section], grad_blocks, precision=lax.Precision.HIGHEST)
        both_sides = jnp.einsum("cahd,hde->cahe", left_side.reshape(NBLK, BLK, KVH, HD), inv_head[section], precision=lax.Precision.HIGHEST)
        precond_list.append(both_sides.reshape(NBLK, BLK, KVH * HD))
    passed = jnp.stack(sent_list[1:] + [jnp.zeros((TOKENS, D), jnp.bfloat16)])
    return passed, jnp.stack(precond_list), jnp.stack(input_list), jnp.stack(head_list)
```

```python
import jax
import jax.numpy as jnp
from jax import lax
from jax.experimental import pallas as pl
from jax.experimental.pallas import tpu as pltpu
from jax.sharding import PartitionSpec as P

rope_base = 100000.0
AXES = ("segment", "dp")
SECTIONS = 8
NX, NY, NZ = 4, 4, 2
DP = NX * NY * NZ
BLK = 192
HALF = BLK // 2
PAIR = 2 * BLK
KO = 512
HD = 128
KVH = 4
PACK = KO + 128

Z, YA, YB, XA, XB = 0, 1, 2, 3, 4
ORDERS = (
    ((XA, XB, YA, YB), (XB, XA, YB, YA)),
    ((YA, YB, XA, XB), (YB, YA, XB, XA)),
)


def gray(i):
    return i ^ (i >> 1)


def place_bits(dp):
    return (gray(dp >> 3) << 3) | (gray((dp >> 1) & 3) << 1) | (dp & 1)


def flipped(dp, dim):
    x, y, z = dp >> 3, (dp >> 1) & 3, dp & 1
    if dim == XA:
        x ^= 1
    elif dim == XB:
        x = 3 - x
    elif dim == YA:
        y ^= 1
    elif dim == YB:
        y = 3 - y
    else:
        z ^= 1
    return (x * NY + y) * NZ + z


def swap_route(stream, step):
    route = []
    for seg in range(SECTIONS):
        dim = Z if step == 4 else ORDERS[seg % 2][stream][step]
        for dp in range(DP):
            route.append((seg * DP + dp, seg * DP + flipped(dp, dim)))
    return route


def back_route(cross):
    route = []
    for seg in range(1, SECTIONS):
        for dp in range(DP):
            target = flipped(dp, Z) if cross else dp
            route.append((seg * DP + dp, (seg - 1) * DP + target))
    return route


def bit(v, i):
    return (v >> i) & 1


def stream_place(rel, core, stream, weights):
    even, odd = ORDERS[0][stream], ORDERS[1][stream]
    on_even = sum(bit(rel, d) * w for d, w in zip(even, weights))
    on_odd = sum(bit(rel, d) * w for d, w in zip(odd, weights))
    return jnp.where(core == 0, on_even, on_odd)


def fim_positions(token_index, bounds, total):
    prefix_len = bounds[0]
    suffix_len = bounds[1]
    middle_len = total - prefix_len - suffix_len
    return jnp.where(
        token_index < prefix_len,
        token_index,
        jnp.where(
            token_index < prefix_len + suffix_len,
            token_index + middle_len,
            token_index - suffix_len,
        ),
    )


def rope_back(grad_rot, token_pos, head_count, head_dim):
    half_dim = head_dim // 2
    frequency = jnp.power(
        jnp.float32(rope_base), -2.0 * jnp.arange(half_dim, dtype=jnp.float32) / head_dim
    )
    angle = token_pos.astype(jnp.float32)[:, None] * frequency[None, :]
    cosines = jnp.cos(angle)
    sines = jnp.sin(angle)
    cos_wide = jnp.tile(cosines, (1, 2 * head_count))
    sin_wide = jnp.tile(jnp.concatenate([sines, -sines], axis=1), (1, head_count))
    grad = grad_rot.astype(jnp.float32)
    rows = grad.shape[0]
    heads = grad.reshape(rows, head_count, 2, half_dim)
    swapped = jnp.concatenate([heads[:, :, 1:], heads[:, :, :1]], axis=2).reshape(grad.shape)
    return grad * cos_wide + swapped * sin_wide


def dot_rows(a, b):
    return lax.dot_general(a, b, (((0,), (0,)), ((), ())), preferred_element_type=jnp.float32)


def products_kernel(slot_ref, x_ref, k_ref, send_a, keep_a, send_b, keep_b, head_ref, place):
    core = lax.axis_index("segment") & 1
    me = place_bits(lax.axis_index("dp"))
    for j in range(DP):
        rel = me ^ place_bits(j)
        block = slot_ref[j]
        for stream in range(2):
            place[stream, block] = stream_place(rel, core, stream, (16, 8, 4, 2)) + bit(rel, Z)
    keys = k_ref[...]
    for h in range(KVH):
        head = keys[:, h * HD : (h + 1) * HD]
        head_ref[h] = dot_rows(head, head)
    half = DP // 2

    def put(stream, send, keep, block, wide, narrow):
        at = place[stream, block]

        @pl.when(at >= half)
        def _():
            send[at - half, :, :KO] = wide.astype(jnp.bfloat16)
            send[at - half, :, KO:] = narrow.astype(jnp.bfloat16)

        @pl.when(at < half)
        def _():
            keep[at, :, :KO] = wide
            keep[at, :, KO:] = narrow

    def pair(q, _):
        cols = x_ref[:, pl.ds(pl.multiple_of(q * PAIR, 128), PAIR)]
        for e in range(2):
            own = cols[:, e * BLK : (e + 1) * BLK]
            wide = dot_rows(own, keys)
            gram = dot_rows(own, own)
            top = jnp.concatenate([gram[:64, :64], gram[128:, 128:]], axis=1)
            narrow = jnp.concatenate([top, gram[64:, :128]], axis=0)
            put(0, send_a, keep_a, 2 * q + e, wide[:HALF], narrow[:HALF])
            put(1, send_b, keep_b, 2 * q + e, wide[HALF:], narrow[HALF:])
        return 0

    lax.fori_loop(0, DP // 2, pair, 0)


def section_products(slots, inputs_local, key_pre):
    half = DP // 2
    send = jax.ShapeDtypeStruct((half, HALF, PACK), jnp.bfloat16)
    keep = jax.ShapeDtypeStruct((half, HALF, PACK), jnp.float32)
    vmem = pl.BlockSpec(memory_space=pltpu.VMEM)
    return pl.pallas_call(
        products_kernel,
        out_shape=(send, keep, send, keep, jax.ShapeDtypeStruct((KVH, HD, HD), jnp.float32)),
        in_specs=[pl.BlockSpec(memory_space=pltpu.SMEM), vmem, vmem],
        out_specs=(vmem,) * 5,
        scratch_shapes=[pltpu.SMEM((2, DP), jnp.int32)],
        compiler_params=pltpu.CompilerParams(vmem_limit_bytes=40 * 2**20),
        cost_estimate=pl.CostEstimate(
            flops=2 * 256 * 6144 * 704, bytes_accessed=20 * 2**20, transcendentals=0
        ),
        name="section_products",
    )(slots, inputs_local, key_pre)


def finish_kernel(total, keep_a, got_a, keep_b, got_b, inv_in, inv_out, precond_ref, gram_ref, left):
    scale = jnp.float32(1.0 / total)
    sum_a = (keep_a[0] + got_a[0].astype(jnp.float32)) * scale
    sum_b = (keep_b[0] + got_b[0].astype(jnp.float32)) * scale
    left[...] = jnp.concatenate([sum_a[:, :KO], sum_b[:, :KO]], axis=0)
    packed = jnp.concatenate([sum_a[:, KO:], sum_b[:, KO:]], axis=0)
    low = packed[64:]
    turned = low.T
    gram_ref[:64] = jnp.concatenate([packed[:64, :64], turned[:64]], axis=1)
    gram_ref[64:128] = jnp.concatenate([low[:64], turned[64:, 64:]], axis=1)
    gram_ref[128:] = jnp.concatenate([low[64:], packed[:64, 64:]], axis=1)
    left[...] = jnp.dot(
        inv_in[0],
        left[...],
        precision=lax.Precision.HIGHEST,
        preferred_element_type=jnp.float32,
    )
    for h in range(KVH):
        cols = slice(h * HD, (h + 1) * HD)
        precond_ref[0, :, cols] = jnp.dot(
            left[:, cols],
            inv_out[h],
            precision=lax.Precision.HIGHEST,
            preferred_element_type=jnp.float32,
        )


def finished(total, keep_a, got_a, keep_b, got_b, inv_in, inv_out):
    vmem = pl.BlockSpec(memory_space=pltpu.VMEM)

    def kernel(*refs):
        finish_kernel(total, *refs)

    return pl.pallas_call(
        kernel,
        out_shape=(
            jax.ShapeDtypeStruct((1, BLK, KO), jnp.float32),
            jax.ShapeDtypeStruct((BLK, BLK), jnp.float32),
        ),
        in_specs=[vmem] * 6,
        out_specs=(vmem, vmem),
        scratch_shapes=[pltpu.VMEM((BLK, KO), jnp.float32)],
        compiler_params=pltpu.CompilerParams(vmem_limit_bytes=16 * 2**20),
        name="finish",
    )(keep_a, got_a, keep_b, got_b, inv_in, inv_out)


def passed_kernel(held_a, got_a, held_b, got_b, k_ref, resid_ref, out_ref, partial):
    core = lax.axis_index("segment") & 1
    me = place_bits(lax.axis_index("dp"))
    lower = len(ORDERS[0][0])
    inv_gray = gray

    def column(stream, h):
        even, odd = ORDERS[0][stream], ORDERS[1][stream]
        on_even = sum(bit(h, i) << even[i] for i in range(lower))
        on_odd = sum(bit(h, i) << odd[i] for i in range(lower))
        owner = me ^ jnp.where(core == 0, on_even, on_odd)
        x = inv_gray(owner >> 3)
        y = inv_gray((owner >> 1) & 3)
        return pl.ds(pl.multiple_of((x * NY + y) * PAIR, 128), PAIR)

    def times(keys, rows):
        return lax.dot_general(
            keys, rows, (((1,), (1,)), ((), ())), preferred_element_type=jnp.float32
        )

    keys = k_ref[:, : KO // 2]
    for ref, base in ((held_a, 0), (got_a, 8)):

        def first(h, _, ref=ref, base=base):
            partial[:, column(0, h + base)] = times(keys, ref[h])
            return 0

        lax.fori_loop(0, 8, first, 0)
    more_keys = k_ref[:, KO // 2 :]
    for ref, base in ((held_b, 0), (got_b, 8)):

        def second(h, _, ref=ref, base=base):
            cols = column(1, h + base)
            branch = partial[:, cols] + times(more_keys, ref[h])
            out_ref[:, cols] = (resid_ref[:, cols].astype(jnp.float32) + branch).astype(
                jnp.bfloat16
            )
            return 0

        lax.fori_loop(0, 8, second, 0)


def passed_grad(held_a, got_a, held_b, got_b, key_pre, resid):
    vmem = pl.BlockSpec(memory_space=pltpu.VMEM)
    return pl.pallas_call(
        passed_kernel,
        out_shape=jax.ShapeDtypeStruct(resid.shape, jnp.bfloat16),
        in_specs=[vmem] * 6,
        out_specs=vmem,
        scratch_shapes=[pltpu.VMEM(resid.shape, jnp.float32)],
        compiler_params=pltpu.CompilerParams(vmem_limit_bytes=40 * 2**20),
        cost_estimate=pl.CostEstimate(
            flops=2 * 256 * 6144 * 512, bytes_accessed=12 * 2**20, transcendentals=0
        ),
        name="passed_grad",
    )(held_a, got_a, held_b, got_b, key_pre, resid)


def hop(block, route):
    return lax.ppermute(block, AXES, route)


def body(
    layer_inputs, resid_grad, key_grad, key_weight, fim_bounds, slot_block, inv_input, inv_head
):
    inputs_local = layer_inputs[0]
    row_count = inputs_local.shape[0]
    total = row_count * lax.axis_size("dp")
    dp = lax.axis_index("dp")

    straight = hop(key_weight[0], back_route(False))
    crossed = hop(key_weight[0], back_route(True))

    token_index = dp * row_count + jnp.arange(row_count, dtype=jnp.int32)
    token_pos = fim_positions(token_index, fim_bounds[0], total)
    key_pre = rope_back(key_grad[0], token_pos, KVH, HD).astype(jnp.bfloat16)

    send_a, keep_a, send_b, keep_b, head_sum = section_products(
        slot_block[0], inputs_local, key_pre
    )

    even = (dp & 1) == 0
    pair = jnp.concatenate(
        [jnp.where(even, straight, crossed), jnp.where(even, crossed, straight)], axis=0
    )
    held = [pair[None, :, : KO // 2], pair[None, :, KO // 2 :]]

    resid_in, key_in, pair = lax.optimization_barrier((resid_grad[0], key_pre, pair))
    resid = hop(resid_in, back_route(False))
    key_next = hop(key_in, back_route(False))

    sends, keeps = [send_a, send_b], [keep_a, keep_b]
    got = [None, None]
    came = [None, None]
    for step in range(5):
        rounded = lax.reduce_precision(head_sum, 8, 7)
        other = hop(rounded.astype(jnp.bfloat16), swap_route(0, (step + 4) % 5))
        head_sum = rounded + other.astype(jnp.float32)
        for s in range(2):
            if step < 4:
                came[s] = hop(held[s], swap_route(s, step))
                if step < 3:
                    held[s] = jnp.concatenate([held[s], came[s]], axis=0)
        for s in range(2):
            got[s] = hop(sends[s], swap_route(s, step))
            if step < 4:
                summed = keeps[s] + got[s].astype(jnp.float32)
                left = summed.shape[0] // 2
                keeps[s] = summed[:left]
                sends[s] = summed[left:].astype(jnp.bfloat16)

    passed = passed_grad(held[0], came[0], held[1], came[1], key_next, resid)
    precond, gram = finished(
        total, keeps[0], got[0], keeps[1], got[1], inv_input[0], inv_head[0]
    )
    head_grams = head_sum / total
    return (passed[None], precond[None], gram[None, None], head_grams[None])


def solution(mesh):
    return jax.shard_map(
        body,
        mesh=mesh,
        in_specs=(
            P("segment", "dp", None),
            P("segment", "dp", None),
            P("segment", "dp", None),
            P("segment", "dp", None),
            P("segment", None),
            P("segment", None),
            P("segment", "dp", None, None),
            P("segment", None, None, None),
        ),
        out_specs=(
            P("segment", "dp", None),
            P("segment", "dp", None, None),
            P("segment", "dp", None, None),
            P("segment", None, None, None),
        ),
        check_vma=False,
    )
```

```python
import jax
import jax.numpy as jnp
from jax import lax
from jax.experimental import pallas as pl
from jax.experimental.pallas import tpu as pltpu
from jax.sharding import PartitionSpec as P

rope_base = 100000.0
AXES = ("segment", "dp")
SECTIONS = 8
NX, NY, NZ = 4, 4, 2
DP = NX * NY * NZ
BLK = 192
PAIR = 2 * BLK
KO = 512
HD = 128
KVH = 4
CUT = 120
FOLD = 48

Z, YA, YB, XA, XB = 0, 1, 2, 3, 4
SUMS = (
    ((XA, XB, YA, YB, Z), (XB, XA, YA, YB, Z)),
    ((YA, YB, XA, XB, Z), (YB, YA, XA, XB, Z)),
)
WEIGHTS = (
    ((XA, XB, YA, YB), (XA, XB, YB, YA)),
    ((YA, YB, XA, XB), (YA, YB, XB, XA)),
)
RINGS = (((XA, XB), (YA, YB)), ((YA, YB), (XA, XB)))


def gray(i):
    return i ^ (i >> 1)


def place_bits(dp):
    return (gray(dp >> 3) << 3) | (gray((dp >> 1) & 3) << 1) | (dp & 1)


def flipped(dp, dim):
    x, y, z = dp >> 3, (dp >> 1) & 3, dp & 1
    if dim == XA:
        x ^= 1
    elif dim == XB:
        x = 3 - x
    elif dim == YA:
        y ^= 1
    elif dim == YB:
        y = 3 - y
    else:
        z ^= 1
    return (x * NY + y) * NZ + z


def flip_route(dims_of_core, sections=SECTIONS):
    route = []
    for seg in range(sections):
        for dp in range(DP):
            target = dp
            for dim in dims_of_core[seg % 2]:
                target = flipped(target, dim)
            route.append((seg * DP + dp, seg * DP + target))
    return route


def step_route(orders, stream, step):
    sections = SECTIONS - 1 if orders is WEIGHTS else SECTIONS
    return flip_route([(orders[core][stream][step],) for core in range(2)], sections)


def ring_route(ring, which):
    dims = [RINGS[core][ring] for core in range(2)]
    return flip_route([[d for i, d in enumerate(pair) if bit(which, i)] for pair in dims])


def back_route(cross):
    route = []
    for seg in range(1, SECTIONS):
        for dp in range(DP):
            target = flipped(dp, Z) if cross else dp
            route.append((seg * DP + dp, (seg - 1) * DP + target))
    return route


def bit(v, i):
    return (v >> i) & 1


def dot_rows(a, b):
    return lax.dot_general(a, b, (((0,), (0,)), ((), ())), preferred_element_type=jnp.float32)


def dot_cols(a, b):
    return lax.dot_general(a, b, (((1,), (1,)), ((), ())), preferred_element_type=jnp.float32)


def dot(a, b):
    return jnp.dot(a, b, preferred_element_type=jnp.float32)


def my_place():
    return lax.axis_index("segment") & 1, place_bits(lax.axis_index("dp"))


def block_order(slot_ref, order_ref):
    core, me = my_place()
    for stream in range(2):
        for r in range(DP):
            rels = [
                sum(bit(r, 4 - k) << d for k, d in enumerate(SUMS[c][stream])) for c in range(2)
            ]
            owner = me ^ jnp.where(core == 0, rels[0], rels[1])
            x, y, z = gray(owner >> 3), gray((owner >> 1) & 3), owner & 1
            order_ref[stream, r] = slot_ref[0, (x * NY + y) * NZ + z]


def frequencies():
    lane = lax.broadcasted_iota(jnp.int32, (1, HD), 1) & (HD // 2 - 1)
    row = jnp.full((1, HD), 1.0, jnp.float32)
    for i in range(1, HD // 2):
        row = jnp.where(lane == i, jnp.float32(rope_base ** (-2.0 * i / HD)), row)
    return row


def rope_back(grad_ref, bounds_ref, key_ref, total):
    rows = grad_ref.shape[1]
    index = lax.axis_index("dp") * rows + lax.broadcasted_iota(jnp.int32, (rows, HD), 0)
    prefix_len, suffix_len = bounds_ref[0, 0], bounds_ref[0, 1]
    position = jnp.where(
        index < prefix_len,
        index,
        jnp.where(
            index < prefix_len + suffix_len,
            index + (total - prefix_len - suffix_len),
            index - suffix_len,
        ),
    )
    angle = position.astype(jnp.float32) * frequencies()
    cosines = jnp.cos(angle)
    sines = jnp.sin(angle)
    lane = lax.broadcasted_iota(jnp.int32, (rows, HD), 1)
    sines = jnp.where(lane < HD // 2, sines, -sines)
    for h in range(KVH):
        cols = slice(h * HD, (h + 1) * HD)
        grad = grad_ref[0, :, cols].astype(jnp.float32)
        swapped = pltpu.roll(grad, HD // 2, 1)
        key_ref[:, cols] = (grad * cosines + swapped * sines).astype(jnp.bfloat16)


def keys_kernel(
    total, slot_ref, bounds_ref, grad_ref, weight_ref, key_ref, head_ref, order_ref, both_ref
):
    block_order(slot_ref, order_ref)
    rope_back(grad_ref, bounds_ref, key_ref, total)
    for h in range(KVH):
        head = key_ref[:, h * HD : (h + 1) * HD]
        head_ref[h * HD : (h + 1) * HD] = dot_rows(head, head).astype(jnp.bfloat16)
    both_ref[:BLK] = weight_ref[0]
    both_ref[BLK:] = key_ref[...]


def keys_and_order(total, slots, bounds, key_grad, key_weight):
    rows = key_grad.shape[1]
    smem = pl.BlockSpec(memory_space=pltpu.SMEM)
    vmem = pl.BlockSpec(memory_space=pltpu.VMEM)

    def kernel(*refs):
        keys_kernel(total, *refs)

    return pl.pallas_call(
        kernel,
        out_shape=(
            jax.ShapeDtypeStruct((rows, KO), jnp.bfloat16),
            jax.ShapeDtypeStruct((KVH * HD, HD), jnp.bfloat16),
            jax.ShapeDtypeStruct((2, DP), jnp.int32),
            jax.ShapeDtypeStruct((BLK + rows, KO), jnp.bfloat16),
        ),
        in_specs=[smem, smem, vmem, vmem],
        out_specs=(vmem, vmem, smem, vmem),
        compiler_params=pltpu.CompilerParams(vmem_limit_bytes=8 * 2**20),
        name="keys",
    )(slots, bounds, key_grad, key_weight)


def products_loop(order_ref, x_ref, key_ref, turned, out_a, out_b, base):
    lane = lax.broadcasted_iota(jnp.int32, (64, 128), 1)
    lower = lane < 64

    def one(i, _):
        block = order_ref[0, base + i]
        rows = turned[pl.ds(pl.multiple_of(block * BLK, 64), CUT)]
        out_a[i] = dot(rows, key_ref[...]).astype(out_a.dtype)

        block = order_ref[1, base + i]
        odd = block & 1
        rows = turned[pl.ds(pl.multiple_of(block * BLK, 64), BLK)]
        out_b[i, : BLK - CUT] = dot(rows[CUT:], key_ref[...]).astype(out_b.dtype)
        window = pl.multiple_of((block >> 1) * PAIR + odd * 128, 128)
        gram = dot(rows, x_ref[0, :, pl.ds(window, 256)])
        near, far = gram[:, :128], gram[:, 128:]
        even_top = jnp.where(lower, near[:64], pltpu.roll(far[128:], 64, 1))
        odd_end = jnp.where(lower, pltpu.roll(near[:64], 64, 1), far[128:])
        is_odd = odd == 1
        packed = jnp.concatenate(
            [
                jnp.where(is_odd, far[:64], even_top),
                jnp.where(is_odd, far[64:128], near[64:128]),
                jnp.where(is_odd, odd_end, near[128:]),
            ],
            axis=0,
        )
        for c in range(4):
            part = packed[c * FOLD : (c + 1) * FOLD].astype(out_b.dtype)
            out_b[i, BLK - CUT :, c * 128 : (c + 1) * 128] = part
        return 0

    lax.fori_loop(0, out_a.shape[0], one, 0, unroll=4)


def sent_kernel(order_ref, x_ref, key_ref, send_a, send_b, turned):
    for c in range(DP // 4):
        wide = slice(c * 4 * BLK, (c + 1) * 4 * BLK)
        turned[wide] = x_ref[0, :, wide].T
    products_loop(order_ref, x_ref, key_ref, turned, send_a, send_b, DP // 2)


def kept_kernel(order_ref, x_ref, key_ref, turned, far_a, far_b, near_a, near_b):
    products_loop(order_ref, x_ref, key_ref, turned, far_a, far_b, DP // 4)
    products_loop(order_ref, x_ref, key_ref, turned, near_a, near_b, 0)


SEND = jax.ShapeDtypeStruct((DP // 2, CUT, KO), jnp.bfloat16)
KEEP = jax.ShapeDtypeStruct((DP // 4, CUT, KO), jnp.float32)
NEXT = jax.ShapeDtypeStruct((DP // 4, CUT, KO), jnp.bfloat16)


def products(kernel, name, out_shape, *args):
    smem = pl.BlockSpec(memory_space=pltpu.SMEM)
    vmem = pl.BlockSpec(memory_space=pltpu.VMEM)
    return pl.pallas_call(
        kernel,
        out_shape=out_shape,
        in_specs=[smem] + [vmem] * (len(args) - 1),
        out_specs=(vmem,) * len(out_shape),
        compiler_params=pltpu.CompilerParams(vmem_limit_bytes=24 * 2**20),
        cost_estimate=pl.CostEstimate(
            flops=256 * 6144 * 704, bytes_accessed=10 * 2**20, transcendentals=0
        ),
        name=name,
    )(*args)


def sent_products(order, layer_inputs, key_pre):
    rows, width = layer_inputs.shape[1:]
    turned = jax.ShapeDtypeStruct((width, rows), jnp.bfloat16)
    return products(
        sent_kernel, "sent_products", (SEND, SEND, turned), order, layer_inputs, key_pre
    )


def kept_products(order, layer_inputs, key_pre, turned):
    return products(
        kept_kernel, "kept_products", (KEEP,) * 4, order, layer_inputs, key_pre, turned
    )


def halved_kernel(far_a, got_a, far_b, got_b, send_a, send_b):
    for far, got, send in ((far_a, got_a, send_a), (far_b, got_b, send_b)):
        for i in range(8):
            send[i] = (far[i] + got[8 + i].astype(jnp.float32)).astype(jnp.bfloat16)


def halved(far_a, got_a, far_b, got_b):
    vmem = pl.BlockSpec(memory_space=pltpu.VMEM)
    return pl.pallas_call(
        halved_kernel,
        out_shape=(NEXT, NEXT),
        in_specs=[vmem] * 4,
        out_specs=(vmem,) * 2,
        compiler_params=pltpu.CompilerParams(vmem_limit_bytes=16 * 2**20),
        name="halved",
    )(far_a, got_a, far_b, got_b)


RING_ROWS = 4 * CUT


def ring_sums_kernel(near_a, first_a, got_a, near_b, first_b, got_b, head, own, to_a, to_b, to_ab):
    groups = ((near_a, first_a, got_a), (near_b, first_b, got_b))
    for s, (near, first, got) in enumerate(groups):
        for i in range(8):
            total = near[i] + first[i].astype(jnp.float32) + got[i].astype(jnp.float32)
            out = (own, to_b, to_a, to_ab)[i // 2]
            row = (s * 2 + i % 2) * CUT
            out[row : row + CUT] = total.astype(out.dtype)
    for out in (to_a, to_b, to_ab):
        out[RING_ROWS:] = head[...]


def ring_sums(*parts):
    vmem = pl.BlockSpec(memory_space=pltpu.VMEM)
    sent = jax.ShapeDtypeStruct((RING_ROWS + HD, KO), jnp.bfloat16)
    return pl.pallas_call(
        ring_sums_kernel,
        out_shape=(jax.ShapeDtypeStruct((RING_ROWS, KO), jnp.float32), sent, sent, sent),
        in_specs=[vmem] * 7,
        out_specs=(vmem,) * 4,
        compiler_params=pltpu.CompilerParams(vmem_limit_bytes=20 * 2**20),
        name="ring_sums",
    )(*parts)


def last_sums_kernel(total, own, head, got_a, got_b, got_ab, keep, send, head_ref):
    def added(mine, rows):
        terms = [got[rows].astype(jnp.float32) for got in (got_a, got_b, got_ab)]
        return (mine + terms[0]) + (terms[1] + terms[2])

    for s in range(2):
        for i, out in enumerate((send, keep)):
            row = (s * 2 + 1 - i) * CUT
            rows = slice(row, row + CUT)
            out[s] = added(own[rows], rows).astype(out.dtype)
    heads = added(head[...].astype(jnp.float32), slice(RING_ROWS, RING_ROWS + HD))
    for h in range(KVH):
        head_ref[0, h] = heads[:, h * HD : (h + 1) * HD] * jnp.float32(1.0 / total)


def last_sums(total, *parts):
    vmem = pl.BlockSpec(memory_space=pltpu.VMEM)
    shape = (2, CUT, KO)

    def kernel(*refs):
        last_sums_kernel(total, *refs)

    return pl.pallas_call(
        kernel,
        out_shape=(
            jax.ShapeDtypeStruct(shape, jnp.float32),
            jax.ShapeDtypeStruct(shape, jnp.bfloat16),
            jax.ShapeDtypeStruct((1, KVH, HD, HD), jnp.float32),
        ),
        in_specs=[vmem] * 5,
        out_specs=(vmem,) * 3,
        compiler_params=pltpu.CompilerParams(vmem_limit_bytes=8 * 2**20),
        name="last_sums",
    )(*parts)


def pair_kernel(straight, crossed, head, other, out):
    first = lax.axis_index("dp") & 1

    def turn(top, bottom):
        out[:, :PAIR] = jnp.concatenate([top[:BLK], bottom[:BLK]], axis=0).T

    pl.when(first == 0)(lambda: turn(straight, crossed))
    pl.when(first == 1)(lambda: turn(crossed, straight))
    both = head[...].astype(jnp.float32) + other[...].astype(jnp.float32)
    out[:, PAIR:] = both.astype(jnp.bfloat16)


def weight_pair(straight, crossed, head, other):
    vmem = pl.BlockSpec(memory_space=pltpu.VMEM)
    return pl.pallas_call(
        pair_kernel,
        out_shape=jax.ShapeDtypeStruct((KO, PAIR + HD), jnp.bfloat16),
        in_specs=[vmem] * 4,
        out_specs=vmem,
        compiler_params=pltpu.CompilerParams(vmem_limit_bytes=8 * 2**20),
        name="weight_pair",
    )(straight, crossed, head, other)


def stack_kernel(own, near_a, near_b, near_ab, held_a, held_b, head):
    pieces = (own, near_a, near_b, near_ab)
    for i, piece in enumerate(pieces):
        held_a[i] = piece[: KO // 2, :PAIR]
        held_b[i] = piece[KO // 2 :, :PAIR]
    terms = [piece[:, PAIR:].astype(jnp.float32) for piece in pieces]
    total = ((terms[0] + terms[1]) + (terms[2] + terms[3])).astype(jnp.bfloat16)
    for h in range(KVH):
        head[:, h * HD : (h + 1) * HD] = total[h * HD : (h + 1) * HD]


def stacked(pieces):
    vmem = pl.BlockSpec(memory_space=pltpu.VMEM)
    held = jax.ShapeDtypeStruct((4, KO // 2, PAIR), jnp.bfloat16)
    return pl.pallas_call(
        stack_kernel,
        out_shape=(held, held, jax.ShapeDtypeStruct((HD, KO), jnp.bfloat16)),
        in_specs=[vmem] * 4,
        out_specs=(vmem,) * 3,
        compiler_params=pltpu.CompilerParams(vmem_limit_bytes=8 * 2**20),
        name="stacked",
    )(*pieces)


def finish_kernel(total, slot_ref, keep, got, inv_in, inv_out, precond_ref, gram_ref):
    scale = jnp.float32(1.0 / total)
    sum_a = (keep[0] + got[0].astype(jnp.float32)) * scale
    sum_b = (keep[1] + got[1].astype(jnp.float32)) * scale
    grad = jnp.concatenate([sum_a, sum_b[: BLK - CUT]], axis=0)
    packed = jnp.concatenate(
        [sum_b[BLK - CUT :, c * 128 : (c + 1) * 128] for c in range(4)], axis=0
    )
    odd = slot_ref[0, lax.axis_index("dp")] & 1

    @pl.when(odd == 0)
    def _():
        low = packed[64:]
        turned = low.T
        gram_ref[:64] = jnp.concatenate([packed[:64, :64], turned[:64]], axis=1)
        gram_ref[64:128] = jnp.concatenate([low[:64], turned[64:, 64:]], axis=1)
        gram_ref[128:] = jnp.concatenate([low[64:], packed[:64, 64:]], axis=1)

    @pl.when(odd == 1)
    def _():
        high = packed[:128]
        turned = high.T
        gram_ref[:64] = jnp.concatenate([packed[128:, :64], high[:64]], axis=1)
        gram_ref[64:128] = jnp.concatenate([turned[:64, :64], high[64:]], axis=1)
        gram_ref[128:] = jnp.concatenate([turned[64:], packed[128:, 64:]], axis=1)

    for h in range(KVH):
        cols = slice(h * HD, (h + 1) * HD)
        left = jnp.dot(
            inv_in[0],
            grad[:, cols],
            precision=lax.Precision.HIGHEST,
            preferred_element_type=jnp.float32,
        )
        precond_ref[0, :, cols] = jnp.dot(
            left,
            inv_out[h],
            precision=lax.Precision.HIGHEST,
            preferred_element_type=jnp.float32,
        )


def finished(total, slots, keep, got, inv_in, inv_out):
    vmem = pl.BlockSpec(memory_space=pltpu.VMEM)

    def kernel(*refs):
        finish_kernel(total, *refs)

    return pl.pallas_call(
        kernel,
        out_shape=(
            jax.ShapeDtypeStruct((1, BLK, KO), jnp.float32),
            jax.ShapeDtypeStruct((BLK, BLK), jnp.float32),
        ),
        in_specs=[pl.BlockSpec(memory_space=pltpu.SMEM)] + [vmem] * 4,
        out_specs=(vmem, vmem),
        compiler_params=pltpu.CompilerParams(vmem_limit_bytes=16 * 2**20),
        name="finish",
    )(slots, keep, got, inv_in, inv_out)


def passed_block(k_ref, resid_ref, pieces, i, ring):
    core, me = my_place()
    rels = [
        sum(bit(i, k) << d for k, d in enumerate(RINGS[c][0]))
        + sum(bit(ring, k) << d for k, d in enumerate(RINGS[c][1]))
        for c in range(2)
    ]
    owner = me ^ jnp.where(core == 0, rels[0], rels[1])
    x, y = gray(owner >> 3), gray((owner >> 1) & 3)
    cols = pl.ds(pl.multiple_of((x * NY + y) * PAIR, 128), PAIR)
    branch = dot(k_ref[BLK:, : KO // 2], pieces[0][i]) + dot(k_ref[BLK:, KO // 2 :], pieces[1][i])
    return cols, (resid_ref[:, cols].astype(jnp.float32) + branch).astype(jnp.bfloat16)


def passed_kernel(held_a, held_b, third_a, third_b, fourth_a, fourth_b, k_ref, resid_ref, out_ref):
    groups = ((held_a, held_b), (third_a, fourth_b), (fourth_a, third_b))
    for ring, pieces in enumerate(groups):
        for i in range(4):
            cols, block = passed_block(k_ref, resid_ref, pieces, i, ring)
            out_ref[:, cols] = block


def passed_grad(*parts):
    vmem = pl.BlockSpec(memory_space=pltpu.VMEM)
    resid = parts[-1]
    return pl.pallas_call(
        passed_kernel,
        out_shape=jax.ShapeDtypeStruct(resid.shape, jnp.bfloat16),
        in_specs=[vmem] * 8,
        out_specs=vmem,
        compiler_params=pltpu.CompilerParams(vmem_limit_bytes=24 * 2**20),
        cost_estimate=pl.CostEstimate(
            flops=2 * 256 * 4608 * 512, bytes_accessed=12 * 2**20, transcendentals=0
        ),
        name="passed_grad",
    )(*parts)


def passed_rest_kernel(both_a, both_b, k_ref, resid_ref, begun, out_ref, blocks, sems):
    copies = []
    for i in range(4):
        cols, blocks[i] = passed_block(k_ref, resid_ref, (both_a, both_b), i, 3)
        copies.append(pltpu.make_async_copy(blocks.at[i], out_ref.at[:, cols], sems.at[i]))
        copies[i].start()
    for copy in copies:
        copy.wait()


def passed_rest(both_a, both_b, key_pre, resid, begun):
    vmem = pl.BlockSpec(memory_space=pltpu.VMEM)
    hbm = pl.BlockSpec(memory_space=pl.ANY)
    return pl.pallas_call(
        passed_rest_kernel,
        out_shape=jax.ShapeDtypeStruct(resid.shape, jnp.bfloat16),
        in_specs=[vmem] * 4 + [hbm],
        out_specs=hbm,
        input_output_aliases={4: 0},
        scratch_shapes=[
            pltpu.VMEM((4, resid.shape[0], PAIR), jnp.bfloat16),
            pltpu.SemaphoreType.DMA((4,)),
        ],
        compiler_params=pltpu.CompilerParams(vmem_limit_bytes=24 * 2**20),
        cost_estimate=pl.CostEstimate(
            flops=2 * 256 * 1536 * 512, bytes_accessed=4 * 2**20, transcendentals=0
        ),
        name="passed_rest",
    )(both_a, both_b, key_pre, resid, begun)


def hop(block, route):
    return lax.ppermute(block, AXES, route)


def tie(*values):
    return lax.optimization_barrier(values)


def body(
    layer_inputs, resid_grad, key_grad, key_weight, fim_bounds, slot_block, inv_input, inv_head
):
    total = layer_inputs.shape[1] * lax.axis_size("dp")

    key_pre, head, order, weight_and_key = keys_and_order(
        total, slot_block, fim_bounds, key_grad, key_weight
    )
    send_a, send_b, turned = sent_products(order, layer_inputs, key_pre)
    straight = hop(weight_and_key, back_route(False))
    send_a, send_b, head, weight = tie(send_a, send_b, head, key_weight[0])
    first = [hop(x, step_route(SUMS, s, 0)) for s, x in enumerate((send_a, send_b))]
    far_a, far_b, near_a, near_b = kept_products(order, layer_inputs, key_pre, turned)
    crossed = hop(weight, back_route(True))
    other = hop(head, flip_route(((Z,), (Z,))))
    pair = weight_pair(straight, crossed, head, other)
    near = [pair] + [hop(pair, ring_route(0, which)) for which in (1, 2, 3)]
    resid_in, pair = tie(resid_grad[0], pair)
    resid = hop(resid_in, back_route(False))

    far_a, far_b, _ = tie(far_a, far_b, pair)
    sums = halved(far_a, first[0], far_b, first[1])
    second = [hop(sums[s], step_route(SUMS, s, 1)) for s in range(2)]

    held_a, held_b, head = stacked(near)
    held = [held_a, held_b]
    third = [hop(held[s], step_route(WEIGHTS, s, 2)) for s in range(2)]
    second[0], second[1], head = tie(*second, head)
    own, *sent = ring_sums(near_a, first[0], second[0], near_b, first[1], second[1], head)
    ring = [hop(sent[i], ring_route(1, i + 1)) for i in range(3)]
    own, held[0], held[1], third[0], third[1], _, _, _ = tie(own, *held, *third, *ring)
    fourth = [hop(held[s], step_route(WEIGHTS, s, 3)) for s in range(2)]
    both = [hop(third[s], step_route(WEIGHTS, s, 3)) for s in range(2)]
    keep, send, head_grams = last_sums(total, own, head, *ring)
    last = hop(send, flip_route(((Z,), (Z,))))
    begun = passed_grad(*held, *third, *fourth, straight, resid)
    last, both[0], both[1] = tie(last, *both)
    passed = passed_rest(*both, straight, resid, begun)
    precond, gram = finished(total, slot_block, keep, last, inv_input[0], inv_head[0])
    return (passed[None], precond[None], gram[None, None], head_grams)


def solution(mesh):
    return jax.shard_map(
        body,
        mesh=mesh,
        in_specs=(
            P("segment", "dp", None),
            P("segment", "dp", None),
            P("segment", "dp", None),
            P("segment", "dp", None),
            P("segment", None),
            P("segment", None),
            P("segment", "dp", None, None),
            P("segment", None, None, None),
        ),
        out_specs=(
            P("segment", "dp", None),
            P("segment", "dp", None, None),
            P("segment", "dp", None, None),
            P("segment", None, None, None),
        ),
        check_vma=False,
    )
```

```python
import jax
import jax.numpy as jnp
from jax import lax
from jax.experimental import pallas as pl
from jax.experimental.pallas import tpu as pltpu
from jax.sharding import PartitionSpec as P

rope_base = 100000.0
AXES = ("segment", "dp")
SECTIONS = 8
NX, NY, NZ = 4, 4, 2
DP = NX * NY * NZ
BLK = 192
PAIR = 2 * BLK
KO = 512
HD = 128
KVH = 4
CUT = 120
FOLD = 48

Z, YA, YB, XA, XB = 0, 1, 2, 3, 4
SUMS = (
    ((XA, XB, YA, YB, Z), (XB, XA, YA, YB, Z)),
    ((YA, YB, XA, XB, Z), (YB, YA, XA, XB, Z)),
)
WEIGHTS = (
    ((XA, XB, YA, YB), (XA, XB, YB, YA)),
    ((YA, YB, XA, XB), (YA, YB, XB, XA)),
)
RINGS = (((XA, XB), (YA, YB)), ((YA, YB), (XA, XB)))


def gray(i):
    return i ^ (i >> 1)


def place_bits(dp):
    return (gray(dp >> 3) << 3) | (gray((dp >> 1) & 3) << 1) | (dp & 1)


def flipped(dp, dim):
    x, y, z = dp >> 3, (dp >> 1) & 3, dp & 1
    if dim == XA:
        x ^= 1
    elif dim == XB:
        x = 3 - x
    elif dim == YA:
        y ^= 1
    elif dim == YB:
        y = 3 - y
    else:
        z ^= 1
    return (x * NY + y) * NZ + z


def flip_route(dims_of_core, sections=SECTIONS):
    route = []
    for seg in range(sections):
        for dp in range(DP):
            target = dp
            for dim in dims_of_core[seg % 2]:
                target = flipped(target, dim)
            route.append((seg * DP + dp, seg * DP + target))
    return route


def step_route(orders, stream, step):
    sections = SECTIONS - 1 if orders is WEIGHTS else SECTIONS
    return flip_route([(orders[core][stream][step],) for core in range(2)], sections)


def ring_route(ring, which):
    dims = [RINGS[core][ring] for core in range(2)]
    return flip_route([[d for i, d in enumerate(pair) if bit(which, i)] for pair in dims])


def back_route(cross):
    route = []
    for seg in range(1, SECTIONS):
        for dp in range(DP):
            target = flipped(dp, Z) if cross else dp
            route.append((seg * DP + dp, (seg - 1) * DP + target))
    return route


def bit(v, i):
    return (v >> i) & 1


def dot_rows(a, b):
    return lax.dot_general(a, b, (((0,), (0,)), ((), ())), preferred_element_type=jnp.float32)


def dot_cols(a, b):
    return lax.dot_general(a, b, (((1,), (1,)), ((), ())), preferred_element_type=jnp.float32)


def dot(a, b):
    return jnp.dot(a, b, preferred_element_type=jnp.float32)


def my_place():
    return lax.axis_index("segment") & 1, place_bits(lax.axis_index("dp"))


def block_order(slot_ref, order_ref):
    core, me = my_place()
    for stream in range(2):
        for r in range(DP):
            rels = [
                sum(bit(r, 4 - k) << d for k, d in enumerate(SUMS[c][stream])) for c in range(2)
            ]
            owner = me ^ jnp.where(core == 0, rels[0], rels[1])
            x, y, z = gray(owner >> 3), gray((owner >> 1) & 3), owner & 1
            order_ref[stream, r] = slot_ref[0, (x * NY + y) * NZ + z]


def frequencies():
    lane = lax.broadcasted_iota(jnp.int32, (1, HD), 1) & (HD // 2 - 1)
    row = jnp.full((1, HD), 1.0, jnp.float32)
    for i in range(1, HD // 2):
        row = jnp.where(lane == i, jnp.float32(rope_base ** (-2.0 * i / HD)), row)
    return row


def rope_back(grad_ref, bounds_ref, key_ref, total):
    rows = grad_ref.shape[1]
    index = lax.axis_index("dp") * rows + lax.broadcasted_iota(jnp.int32, (rows, HD), 0)
    prefix_len, suffix_len = bounds_ref[0, 0], bounds_ref[0, 1]
    position = jnp.where(
        index < prefix_len,
        index,
        jnp.where(
            index < prefix_len + suffix_len,
            index + (total - prefix_len - suffix_len),
            index - suffix_len,
        ),
    )
    angle = position.astype(jnp.float32) * frequencies()
    cosines = jnp.cos(angle)
    sines = jnp.sin(angle)
    lane = lax.broadcasted_iota(jnp.int32, (rows, HD), 1)
    sines = jnp.where(lane < HD // 2, sines, -sines)
    for h in range(KVH):
        cols = slice(h * HD, (h + 1) * HD)
        grad = grad_ref[0, :, cols].astype(jnp.float32)
        swapped = pltpu.roll(grad, HD // 2, 1)
        key_ref[:, cols] = (grad * cosines + swapped * sines).astype(jnp.bfloat16)


def keys_kernel(
    total, slot_ref, bounds_ref, grad_ref, weight_ref, key_ref, head_ref, order_ref, both_ref
):
    block_order(slot_ref, order_ref)
    rope_back(grad_ref, bounds_ref, key_ref, total)
    for h in range(KVH):
        head = key_ref[:, h * HD : (h + 1) * HD]
        head_ref[h * HD : (h + 1) * HD] = dot_rows(head, head).astype(jnp.bfloat16)
    both_ref[:BLK] = weight_ref[0]
    both_ref[BLK:] = key_ref[...]


def keys_and_order(total, slots, bounds, key_grad, key_weight):
    rows = key_grad.shape[1]
    smem = pl.BlockSpec(memory_space=pltpu.SMEM)
    vmem = pl.BlockSpec(memory_space=pltpu.VMEM)

    def kernel(*refs):
        keys_kernel(total, *refs)

    return pl.pallas_call(
        kernel,
        out_shape=(
            jax.ShapeDtypeStruct((rows, KO), jnp.bfloat16),
            jax.ShapeDtypeStruct((KVH * HD, HD), jnp.bfloat16),
            jax.ShapeDtypeStruct((2, DP), jnp.int32),
            jax.ShapeDtypeStruct((BLK + rows, KO), jnp.bfloat16),
        ),
        in_specs=[smem, smem, vmem, vmem],
        out_specs=(vmem, vmem, smem, vmem),
        compiler_params=pltpu.CompilerParams(vmem_limit_bytes=8 * 2**20),
        name="keys",
    )(slots, bounds, key_grad, key_weight)


def products_loop(order_ref, x_ref, key_ref, turned, out_a, out_b, base):
    lane = lax.broadcasted_iota(jnp.int32, (64, 128), 1)
    lower = lane < 64

    def one(i, _):
        block = order_ref[0, base + i]
        rows = turned[pl.ds(pl.multiple_of(block * BLK, 64), CUT)]
        out_a[i] = dot(rows, key_ref[...]).astype(out_a.dtype)

        block = order_ref[1, base + i]
        odd = block & 1
        rows = turned[pl.ds(pl.multiple_of(block * BLK, 64), BLK)]
        out_b[i, : BLK - CUT] = dot(rows[CUT:], key_ref[...]).astype(out_b.dtype)
        window = pl.multiple_of((block >> 1) * PAIR + odd * 128, 128)
        gram = dot(rows, x_ref[0, :, pl.ds(window, 256)])
        near, far = gram[:, :128], gram[:, 128:]
        even_top = jnp.where(lower, near[:64], pltpu.roll(far[128:], 64, 1))
        odd_end = jnp.where(lower, pltpu.roll(near[:64], 64, 1), far[128:])
        is_odd = odd == 1
        packed = jnp.concatenate(
            [
                jnp.where(is_odd, far[:64], even_top),
                jnp.where(is_odd, far[64:128], near[64:128]),
                jnp.where(is_odd, odd_end, near[128:]),
            ],
            axis=0,
        )
        for c in range(4):
            part = packed[c * FOLD : (c + 1) * FOLD].astype(out_b.dtype)
            out_b[i, BLK - CUT :, c * 128 : (c + 1) * 128] = part
        return 0

    lax.fori_loop(0, out_a.shape[0], one, 0, unroll=4)


def sent_kernel(order_ref, x_ref, key_ref, send_a, send_b, turned):
    for c in range(DP // 4):
        wide = slice(c * 4 * BLK, (c + 1) * 4 * BLK)
        turned[wide] = x_ref[0, :, wide].T
    products_loop(order_ref, x_ref, key_ref, turned, send_a, send_b, DP // 2)


def kept_kernel(order_ref, x_ref, key_ref, turned, far_a, far_b, near_a, near_b):
    products_loop(order_ref, x_ref, key_ref, turned, far_a, far_b, DP // 4)
    products_loop(order_ref, x_ref, key_ref, turned, near_a, near_b, 0)


SEND = jax.ShapeDtypeStruct((DP // 2, CUT, KO), jnp.bfloat16)
KEEP = jax.ShapeDtypeStruct((DP // 4, CUT, KO), jnp.float32)
NEXT = jax.ShapeDtypeStruct((DP // 4, CUT, KO), jnp.bfloat16)


def products(kernel, name, out_shape, *args):
    smem = pl.BlockSpec(memory_space=pltpu.SMEM)
    vmem = pl.BlockSpec(memory_space=pltpu.VMEM)
    return pl.pallas_call(
        kernel,
        out_shape=out_shape,
        in_specs=[smem] + [vmem] * (len(args) - 1),
        out_specs=(vmem,) * len(out_shape),
        compiler_params=pltpu.CompilerParams(vmem_limit_bytes=24 * 2**20),
        cost_estimate=pl.CostEstimate(
            flops=256 * 6144 * 704, bytes_accessed=10 * 2**20, transcendentals=0
        ),
        name=name,
    )(*args)


def sent_products(order, layer_inputs, key_pre):
    rows, width = layer_inputs.shape[1:]
    turned = jax.ShapeDtypeStruct((width, rows), jnp.bfloat16)
    return products(
        sent_kernel, "sent_products", (SEND, SEND, turned), order, layer_inputs, key_pre
    )


def kept_products(order, layer_inputs, key_pre, turned):
    return products(
        kept_kernel, "kept_products", (KEEP,) * 4, order, layer_inputs, key_pre, turned
    )


def halved_kernel(far_a, got_a, far_b, got_b, send_a, send_b):
    for far, got, send in ((far_a, got_a, send_a), (far_b, got_b, send_b)):
        for i in range(8):
            send[i] = (far[i] + got[8 + i].astype(jnp.float32)).astype(jnp.bfloat16)


def halved(far_a, got_a, far_b, got_b):
    vmem = pl.BlockSpec(memory_space=pltpu.VMEM)
    return pl.pallas_call(
        halved_kernel,
        out_shape=(NEXT, NEXT),
        in_specs=[vmem] * 4,
        out_specs=(vmem,) * 2,
        compiler_params=pltpu.CompilerParams(vmem_limit_bytes=16 * 2**20),
        name="halved",
    )(far_a, got_a, far_b, got_b)


RING_ROWS = 4 * CUT


def ring_sums_kernel(near_a, first_a, got_a, near_b, first_b, got_b, head, own, to_a, to_b, to_ab):
    groups = ((near_a, first_a, got_a), (near_b, first_b, got_b))
    for s, (near, first, got) in enumerate(groups):
        for i in range(8):
            total = near[i] + first[i].astype(jnp.float32) + got[i].astype(jnp.float32)
            out = (own, to_b, to_a, to_ab)[i // 2]
            row = (s * 2 + i % 2) * CUT
            out[row : row + CUT] = total.astype(out.dtype)
    for out in (to_a, to_b, to_ab):
        out[RING_ROWS:] = head[...]


def ring_sums(*parts):
    vmem = pl.BlockSpec(memory_space=pltpu.VMEM)
    sent = jax.ShapeDtypeStruct((RING_ROWS + HD, KO), jnp.bfloat16)
    return pl.pallas_call(
        ring_sums_kernel,
        out_shape=(jax.ShapeDtypeStruct((RING_ROWS, KO), jnp.float32), sent, sent, sent),
        in_specs=[vmem] * 7,
        out_specs=(vmem,) * 4,
        compiler_params=pltpu.CompilerParams(vmem_limit_bytes=20 * 2**20),
        name="ring_sums",
    )(*parts)


def last_sums_kernel(total, own, head, got_a, got_b, got_ab, keep, send, head_ref):
    def added(mine, rows):
        terms = [got[rows].astype(jnp.float32) for got in (got_a, got_b, got_ab)]
        return (mine + terms[0]) + (terms[1] + terms[2])

    for s in range(2):
        for i, out in enumerate((send, keep)):
            row = (s * 2 + 1 - i) * CUT
            rows = slice(row, row + CUT)
            out[s] = added(own[rows], rows).astype(out.dtype)
    heads = added(head[...].astype(jnp.float32), slice(RING_ROWS, RING_ROWS + HD))
    for h in range(KVH):
        head_ref[0, h] = heads[:, h * HD : (h + 1) * HD] * jnp.float32(1.0 / total)


def last_sums(total, *parts):
    vmem = pl.BlockSpec(memory_space=pltpu.VMEM)
    shape = (2, CUT, KO)

    def kernel(*refs):
        last_sums_kernel(total, *refs)

    return pl.pallas_call(
        kernel,
        out_shape=(
            jax.ShapeDtypeStruct(shape, jnp.float32),
            jax.ShapeDtypeStruct(shape, jnp.bfloat16),
            jax.ShapeDtypeStruct((1, KVH, HD, HD), jnp.float32),
        ),
        in_specs=[vmem] * 5,
        out_specs=(vmem,) * 3,
        compiler_params=pltpu.CompilerParams(vmem_limit_bytes=8 * 2**20),
        name="last_sums",
    )(*parts)


def pair_kernel(straight, crossed, head, other, out):
    first = lax.axis_index("dp") & 1

    def turn(top, bottom):
        out[:, :PAIR] = jnp.concatenate([top[:BLK], bottom[:BLK]], axis=0).T

    pl.when(first == 0)(lambda: turn(straight, crossed))
    pl.when(first == 1)(lambda: turn(crossed, straight))
    both = head[...].astype(jnp.float32) + other[...].astype(jnp.float32)
    out[:, PAIR:] = both.astype(jnp.bfloat16)


def weight_pair(straight, crossed, head, other):
    vmem = pl.BlockSpec(memory_space=pltpu.VMEM)
    return pl.pallas_call(
        pair_kernel,
        out_shape=jax.ShapeDtypeStruct((KO, PAIR + HD), jnp.bfloat16),
        in_specs=[vmem] * 4,
        out_specs=vmem,
        compiler_params=pltpu.CompilerParams(vmem_limit_bytes=8 * 2**20),
        name="weight_pair",
    )(straight, crossed, head, other)


def stack_kernel(own, near_a, near_b, near_ab, held_a, held_b, head):
    pieces = (own, near_a, near_b, near_ab)
    for i, piece in enumerate(pieces):
        held_a[i] = piece[: KO // 2, :PAIR]
        held_b[i] = piece[KO // 2 :, :PAIR]
    terms = [piece[:, PAIR:].astype(jnp.float32) for piece in pieces]
    total = ((terms[0] + terms[1]) + (terms[2] + terms[3])).astype(jnp.bfloat16)
    for h in range(KVH):
        head[:, h * HD : (h + 1) * HD] = total[h * HD : (h + 1) * HD]


def stacked(pieces):
    vmem = pl.BlockSpec(memory_space=pltpu.VMEM)
    held = jax.ShapeDtypeStruct((4, KO // 2, PAIR), jnp.bfloat16)
    return pl.pallas_call(
        stack_kernel,
        out_shape=(held, held, jax.ShapeDtypeStruct((HD, KO), jnp.bfloat16)),
        in_specs=[vmem] * 4,
        out_specs=(vmem,) * 3,
        compiler_params=pltpu.CompilerParams(vmem_limit_bytes=8 * 2**20),
        name="stacked",
    )(*pieces)


def finish_kernel(total, slot_ref, keep, got, inv_in, inv_out, precond_ref, gram_ref):
    scale = jnp.float32(1.0 / total)
    sum_a = (keep[0] + got[0].astype(jnp.float32)) * scale
    sum_b = (keep[1] + got[1].astype(jnp.float32)) * scale
    grad = jnp.concatenate([sum_a, sum_b[: BLK - CUT]], axis=0)
    packed = jnp.concatenate(
        [sum_b[BLK - CUT :, c * 128 : (c + 1) * 128] for c in range(4)], axis=0
    )
    odd = slot_ref[0, lax.axis_index("dp")] & 1

    @pl.when(odd == 0)
    def _():
        low = packed[64:]
        turned = low.T
        gram_ref[:64] = jnp.concatenate([packed[:64, :64], turned[:64]], axis=1)
        gram_ref[64:128] = jnp.concatenate([low[:64], turned[64:, 64:]], axis=1)
        gram_ref[128:] = jnp.concatenate([low[64:], packed[:64, 64:]], axis=1)

    @pl.when(odd == 1)
    def _():
        high = packed[:128]
        turned = high.T
        gram_ref[:64] = jnp.concatenate([packed[128:, :64], high[:64]], axis=1)
        gram_ref[64:128] = jnp.concatenate([turned[:64, :64], high[64:]], axis=1)
        gram_ref[128:] = jnp.concatenate([turned[64:], packed[128:, 64:]], axis=1)

    for h in range(KVH):
        cols = slice(h * HD, (h + 1) * HD)
        left = jnp.dot(
            inv_in[0],
            grad[:, cols],
            precision=lax.Precision.HIGHEST,
            preferred_element_type=jnp.float32,
        )
        precond_ref[0, :, cols] = jnp.dot(
            left,
            inv_out[h],
            precision=lax.Precision.HIGHEST,
            preferred_element_type=jnp.float32,
        )


def finished(total, slots, keep, got, inv_in, inv_out):
    vmem = pl.BlockSpec(memory_space=pltpu.VMEM)

    def kernel(*refs):
        finish_kernel(total, *refs)

    return pl.pallas_call(
        kernel,
        out_shape=(
            jax.ShapeDtypeStruct((1, BLK, KO), jnp.float32),
            jax.ShapeDtypeStruct((BLK, BLK), jnp.float32),
        ),
        in_specs=[pl.BlockSpec(memory_space=pltpu.SMEM)] + [vmem] * 4,
        out_specs=(vmem, vmem),
        compiler_params=pltpu.CompilerParams(vmem_limit_bytes=16 * 2**20),
        name="finish",
    )(slots, keep, got, inv_in, inv_out)


def passed_block(k_ref, resid_ref, pieces, i, ring):
    core, me = my_place()
    rels = [
        sum(bit(i, k) << d for k, d in enumerate(RINGS[c][0]))
        + sum(bit(ring, k) << d for k, d in enumerate(RINGS[c][1]))
        for c in range(2)
    ]
    owner = me ^ jnp.where(core == 0, rels[0], rels[1])
    x, y = gray(owner >> 3), gray((owner >> 1) & 3)
    cols = pl.ds(pl.multiple_of((x * NY + y) * PAIR, 128), PAIR)
    branch = dot(k_ref[BLK:, : KO // 2], pieces[0][i]) + dot(k_ref[BLK:, KO // 2 :], pieces[1][i])
    return cols, (resid_ref[:, cols].astype(jnp.float32) + branch).astype(jnp.bfloat16)


def passed_kernel(held_a, held_b, third_a, third_b, last_a, last_b, k_ref, resid_ref, out_ref):
    fourth_a, fourth_b, both_a, both_b = last_a.at[:4], last_b.at[:4], last_a.at[4:], last_b.at[4:]
    groups = ((held_a, held_b), (third_a, fourth_b), (fourth_a, third_b), (both_a, both_b))
    for ring, pieces in enumerate(groups):
        for i in range(4):
            cols, block = passed_block(k_ref, resid_ref, pieces, i, ring)
            out_ref[:, cols] = block


def passed_grad(*parts):
    vmem = pl.BlockSpec(memory_space=pltpu.VMEM)
    resid = parts[-1]
    return pl.pallas_call(
        passed_kernel,
        out_shape=jax.ShapeDtypeStruct(resid.shape, jnp.bfloat16),
        in_specs=[vmem] * 8,
        out_specs=vmem,
        compiler_params=pltpu.CompilerParams(vmem_limit_bytes=24 * 2**20),
        cost_estimate=pl.CostEstimate(
            flops=2 * 256 * 6144 * 512, bytes_accessed=12 * 2**20, transcendentals=0
        ),
        name="passed_grad",
    )(*parts)


def hop(block, route):
    return lax.ppermute(block, AXES, route)


def tie(*values):
    return lax.optimization_barrier(values)


def body(
    layer_inputs, resid_grad, key_grad, key_weight, fim_bounds, slot_block, inv_input, inv_head
):
    total = layer_inputs.shape[1] * lax.axis_size("dp")

    key_pre, head, order, weight_and_key = keys_and_order(
        total, slot_block, fim_bounds, key_grad, key_weight
    )
    send_a, send_b, turned = sent_products(order, layer_inputs, key_pre)
    straight = hop(weight_and_key, back_route(False))
    send_a, send_b, head, weight = tie(send_a, send_b, head, key_weight[0])
    first = [hop(x, step_route(SUMS, s, 0)) for s, x in enumerate((send_a, send_b))]
    far_a, far_b, near_a, near_b = kept_products(order, layer_inputs, key_pre, turned)
    crossed = hop(weight, back_route(True))
    other = hop(head, flip_route(((Z,), (Z,))))
    crossed, other, far_a, near_a = tie(crossed, other, far_a, near_a)
    pair = weight_pair(straight, crossed, head, other)
    near = [pair] + [hop(pair, ring_route(0, which)) for which in (1, 2, 3)]
    resid_in, pair = tie(resid_grad[0], pair)
    resid = hop(resid_in, back_route(False))

    far_a, far_b, _ = tie(far_a, far_b, pair)
    sums = halved(far_a, first[0], far_b, first[1])
    second = [hop(sums[s], step_route(SUMS, s, 1)) for s in range(2)]

    held_a, held_b, head = stacked(near)
    held = [held_a, held_b]
    third = [hop(held[s], step_route(WEIGHTS, s, 2)) for s in range(2)]
    second[0], second[1], head = tie(*second, head)
    own, *sent = ring_sums(near_a, first[0], second[0], near_b, first[1], second[1], head)
    ring = [hop(sent[i], ring_route(1, i + 1)) for i in range(3)]
    own, held[0], held[1], third[0], third[1], _, _, _ = tie(own, *held, *third, *ring)
    more = [jnp.concatenate([held[s], third[s]], axis=0) for s in range(2)]
    fourth = [hop(more[s], step_route(WEIGHTS, s, 3)) for s in range(2)]
    keep, send, head_grams = last_sums(total, own, head, *ring)
    last = hop(send, flip_route(((Z,), (Z,))))
    passed = passed_grad(*held, *third, *fourth, straight, resid)
    precond, gram = finished(total, slot_block, keep, last, inv_input[0], inv_head[0])
    return (passed[None], precond[None], gram[None, None], head_grams)


def solution(mesh):
    return jax.shard_map(
        body,
        mesh=mesh,
        in_specs=(
            P("segment", "dp", None),
            P("segment", "dp", None),
            P("segment", "dp", None),
            P("segment", "dp", None),
            P("segment", None),
            P("segment", None),
            P("segment", "dp", None, None),
            P("segment", None, None, None),
        ),
        out_specs=(
            P("segment", "dp", None),
            P("segment", "dp", None, None),
            P("segment", "dp", None, None),
            P("segment", None, None, None),
        ),
        check_vma=False,
    )
```

```python
import jax
import jax.numpy as jnp
from jax import lax
from jax.experimental import pallas as pl
from jax.experimental.pallas import tpu as pltpu
from jax.sharding import PartitionSpec as P

rope_base = 100000.0
AXES = ("segment", "dp")
SECTIONS = 8
NX, NY, NZ = 4, 4, 2
DP = NX * NY * NZ
BLK = 192
PAIR = 2 * BLK
KO = 512
HD = 128
KVH = 4
CUT = 120
FOLD = 48

Z, YA, YB, XA, XB = 0, 1, 2, 3, 4
SUMS = (
    ((XA, XB, YA, YB, Z), (XB, XA, YA, YB, Z)),
    ((YA, YB, XA, XB, Z), (YB, YA, XA, XB, Z)),
)
WEIGHTS = (
    ((XA, XB, YA, YB), (XA, XB, YB, YA)),
    ((YA, YB, XA, XB), (YA, YB, XB, XA)),
)
RINGS = (((XA, XB), (YA, YB)), ((YA, YB), (XA, XB)))


def gray(i):
    return i ^ (i >> 1)


def place_bits(dp):
    return (gray(dp >> 3) << 3) | (gray((dp >> 1) & 3) << 1) | (dp & 1)


def flipped(dp, dim):
    x, y, z = dp >> 3, (dp >> 1) & 3, dp & 1
    if dim == XA:
        x ^= 1
    elif dim == XB:
        x = 3 - x
    elif dim == YA:
        y ^= 1
    elif dim == YB:
        y = 3 - y
    else:
        z ^= 1
    return (x * NY + y) * NZ + z


def flip_route(dims_of_core, sections=SECTIONS):
    route = []
    for seg in range(sections):
        for dp in range(DP):
            target = dp
            for dim in dims_of_core[seg % 2]:
                target = flipped(target, dim)
            route.append((seg * DP + dp, seg * DP + target))
    return route


def step_route(orders, stream, step):
    sections = SECTIONS - 1 if orders is WEIGHTS else SECTIONS
    return flip_route([(orders[core][stream][step],) for core in range(2)], sections)


def ring_route(ring, which):
    dims = [RINGS[core][ring] for core in range(2)]
    return flip_route([[d for i, d in enumerate(pair) if bit(which, i)] for pair in dims])


def back_route(cross):
    route = []
    for seg in range(1, SECTIONS):
        for dp in range(DP):
            target = flipped(dp, Z) if cross else dp
            route.append((seg * DP + dp, (seg - 1) * DP + target))
    return route


def bit(v, i):
    return (v >> i) & 1


def dot_rows(a, b):
    return lax.dot_general(a, b, (((0,), (0,)), ((), ())), preferred_element_type=jnp.float32)


def dot_cols(a, b):
    return lax.dot_general(a, b, (((1,), (1,)), ((), ())), preferred_element_type=jnp.float32)


def dot(a, b):
    return jnp.dot(a, b, preferred_element_type=jnp.float32)


def my_place():
    return lax.axis_index("segment") & 1, place_bits(lax.axis_index("dp"))


def block_order(slot_ref, order_ref):
    core, me = my_place()
    for stream in range(2):
        for r in range(DP):
            rels = [
                sum(bit(r, 4 - k) << d for k, d in enumerate(SUMS[c][stream])) for c in range(2)
            ]
            owner = me ^ jnp.where(core == 0, rels[0], rels[1])
            x, y, z = gray(owner >> 3), gray((owner >> 1) & 3), owner & 1
            order_ref[stream, r] = slot_ref[0, (x * NY + y) * NZ + z]


def frequencies():
    lane = lax.broadcasted_iota(jnp.int32, (1, HD), 1) & (HD // 2 - 1)
    row = jnp.full((1, HD), 1.0, jnp.float32)
    for i in range(1, HD // 2):
        row = jnp.where(lane == i, jnp.float32(rope_base ** (-2.0 * i / HD)), row)
    return row


def rope_back(grad_ref, bounds_ref, key_ref, total):
    rows = grad_ref.shape[1]
    index = lax.axis_index("dp") * rows + lax.broadcasted_iota(jnp.int32, (rows, HD), 0)
    prefix_len, suffix_len = bounds_ref[0, 0], bounds_ref[0, 1]
    position = jnp.where(
        index < prefix_len,
        index,
        jnp.where(
            index < prefix_len + suffix_len,
            index + (total - prefix_len - suffix_len),
            index - suffix_len,
        ),
    )
    angle = position.astype(jnp.float32) * frequencies()
    cosines = jnp.cos(angle)
    sines = jnp.sin(angle)
    lane = lax.broadcasted_iota(jnp.int32, (rows, HD), 1)
    sines = jnp.where(lane < HD // 2, sines, -sines)
    for h in range(KVH):
        cols = slice(h * HD, (h + 1) * HD)
        grad = grad_ref[0, :, cols].astype(jnp.float32)
        swapped = pltpu.roll(grad, HD // 2, 1)
        key_ref[:, cols] = (grad * cosines + swapped * sines).astype(jnp.bfloat16)


def keys_kernel(
    total, slot_ref, bounds_ref, grad_ref, weight_ref, key_ref, head_ref, order_ref, both_ref
):
    block_order(slot_ref, order_ref)
    rope_back(grad_ref, bounds_ref, key_ref, total)
    for h in range(KVH):
        head = key_ref[:, h * HD : (h + 1) * HD]
        head_ref[h * HD : (h + 1) * HD] = dot_rows(head, head).astype(jnp.bfloat16)
    both_ref[:BLK] = weight_ref[0]
    both_ref[BLK:] = key_ref[...]


def keys_and_order(total, slots, bounds, key_grad, key_weight):
    rows = key_grad.shape[1]
    smem = pl.BlockSpec(memory_space=pltpu.SMEM)
    vmem = pl.BlockSpec(memory_space=pltpu.VMEM)

    def kernel(*refs):
        keys_kernel(total, *refs)

    return pl.pallas_call(
        kernel,
        out_shape=(
            jax.ShapeDtypeStruct((rows, KO), jnp.bfloat16),
            jax.ShapeDtypeStruct((KVH * HD, HD), jnp.bfloat16),
            jax.ShapeDtypeStruct((2, DP), jnp.int32),
            jax.ShapeDtypeStruct((BLK + rows, KO), jnp.bfloat16),
        ),
        in_specs=[smem, smem, vmem, vmem],
        out_specs=(vmem, vmem, smem, vmem),
        compiler_params=pltpu.CompilerParams(vmem_limit_bytes=8 * 2**20),
        name="keys",
    )(slots, bounds, key_grad, key_weight)


def products_loop(order_ref, x_ref, key_ref, turned, out_a, out_b, base):
    lane = lax.broadcasted_iota(jnp.int32, (64, 128), 1)
    lower = lane < 64

    def one(i, _):
        block = order_ref[0, base + i]
        rows = turned[pl.ds(pl.multiple_of(block * BLK, 64), CUT)]
        out_a[i] = dot(rows, key_ref[...]).astype(out_a.dtype)

        block = order_ref[1, base + i]
        odd = block & 1
        rows = turned[pl.ds(pl.multiple_of(block * BLK, 64), BLK)]
        out_b[i, : BLK - CUT] = dot(rows[CUT:], key_ref[...]).astype(out_b.dtype)
        window = pl.multiple_of((block >> 1) * PAIR + odd * 128, 128)
        gram = dot(rows, x_ref[0, :, pl.ds(window, 256)])
        near, far = gram[:, :128], gram[:, 128:]
        even_top = jnp.where(lower, near[:64], pltpu.roll(far[128:], 64, 1))
        odd_end = jnp.where(lower, pltpu.roll(near[:64], 64, 1), far[128:])
        is_odd = odd == 1
        packed = jnp.concatenate(
            [
                jnp.where(is_odd, far[:64], even_top),
                jnp.where(is_odd, far[64:128], near[64:128]),
                jnp.where(is_odd, odd_end, near[128:]),
            ],
            axis=0,
        )
        for c in range(4):
            part = packed[c * FOLD : (c + 1) * FOLD].astype(out_b.dtype)
            out_b[i, BLK - CUT :, c * 128 : (c + 1) * 128] = part
        return 0

    lax.fori_loop(0, out_a.shape[0], one, 0, unroll=4)


def sent_kernel(order_ref, x_ref, key_ref, send_a, send_b, turned):
    for c in range(DP // 4):
        wide = slice(c * 4 * BLK, (c + 1) * 4 * BLK)
        turned[wide] = x_ref[0, :, wide].T
    products_loop(order_ref, x_ref, key_ref, turned, send_a, send_b, DP // 2)


def kept_kernel(order_ref, x_ref, key_ref, turned, far_a, far_b, near_a, near_b):
    products_loop(order_ref, x_ref, key_ref, turned, far_a, far_b, DP // 4)
    products_loop(order_ref, x_ref, key_ref, turned, near_a, near_b, 0)


SEND = jax.ShapeDtypeStruct((DP // 2, CUT, KO), jnp.bfloat16)
KEEP = jax.ShapeDtypeStruct((DP // 4, CUT, KO), jnp.float32)
NEXT = jax.ShapeDtypeStruct((DP // 4, CUT, KO), jnp.bfloat16)


def products(kernel, name, out_shape, *args):
    smem = pl.BlockSpec(memory_space=pltpu.SMEM)
    vmem = pl.BlockSpec(memory_space=pltpu.VMEM)
    return pl.pallas_call(
        kernel,
        out_shape=out_shape,
        in_specs=[smem] + [vmem] * (len(args) - 1),
        out_specs=(vmem,) * len(out_shape),
        compiler_params=pltpu.CompilerParams(vmem_limit_bytes=24 * 2**20),
        cost_estimate=pl.CostEstimate(
            flops=256 * 6144 * 704, bytes_accessed=10 * 2**20, transcendentals=0
        ),
        name=name,
    )(*args)


def sent_products(order, layer_inputs, key_pre):
    rows, width = layer_inputs.shape[1:]
    turned = jax.ShapeDtypeStruct((width, rows), jnp.bfloat16)
    return products(
        sent_kernel, "sent_products", (SEND, SEND, turned), order, layer_inputs, key_pre
    )


def kept_products(order, layer_inputs, key_pre, turned):
    return products(
        kept_kernel, "kept_products", (KEEP,) * 4, order, layer_inputs, key_pre, turned
    )


def halved_kernel(far_a, got_a, far_b, got_b, send_a, send_b):
    for far, got, send in ((far_a, got_a, send_a), (far_b, got_b, send_b)):
        for i in range(8):
            send[i] = (far[i] + got[8 + i].astype(jnp.float32)).astype(jnp.bfloat16)


def halved(far_a, got_a, far_b, got_b):
    vmem = pl.BlockSpec(memory_space=pltpu.VMEM)
    return pl.pallas_call(
        halved_kernel,
        out_shape=(NEXT, NEXT),
        in_specs=[vmem] * 4,
        out_specs=(vmem,) * 2,
        compiler_params=pltpu.CompilerParams(vmem_limit_bytes=16 * 2**20),
        name="halved",
    )(far_a, got_a, far_b, got_b)


RING_ROWS = 4 * CUT


def ring_sums_kernel(near_a, first_a, got_a, near_b, first_b, got_b, head, own, to_a, to_b, to_ab):
    groups = ((near_a, first_a, got_a), (near_b, first_b, got_b))
    for s, (near, first, got) in enumerate(groups):
        for i in range(8):
            total = near[i] + first[i].astype(jnp.float32) + got[i].astype(jnp.float32)
            out = (own, to_b, to_a, to_ab)[i // 2]
            row = (s * 2 + i % 2) * CUT
            out[row : row + CUT] = total.astype(out.dtype)
    for out in (to_a, to_b, to_ab):
        out[RING_ROWS:] = head[...]


def ring_sums(*parts):
    vmem = pl.BlockSpec(memory_space=pltpu.VMEM)
    sent = jax.ShapeDtypeStruct((RING_ROWS + HD, KO), jnp.bfloat16)
    return pl.pallas_call(
        ring_sums_kernel,
        out_shape=(jax.ShapeDtypeStruct((RING_ROWS, KO), jnp.float32), sent, sent, sent),
        in_specs=[vmem] * 7,
        out_specs=(vmem,) * 4,
        compiler_params=pltpu.CompilerParams(vmem_limit_bytes=20 * 2**20),
        name="ring_sums",
    )(*parts)


def last_sums_kernel(total, own, head, got_a, got_b, got_ab, keep, send, head_ref):
    def added(mine, rows):
        terms = [got[rows].astype(jnp.float32) for got in (got_a, got_b, got_ab)]
        return (mine + terms[0]) + (terms[1] + terms[2])

    for s in range(2):
        for i, out in enumerate((send, keep)):
            row = (s * 2 + 1 - i) * CUT
            rows = slice(row, row + CUT)
            out[s] = added(own[rows], rows).astype(out.dtype)
    heads = added(head[...].astype(jnp.float32), slice(RING_ROWS, RING_ROWS + HD))
    for h in range(KVH):
        head_ref[0, h] = heads[:, h * HD : (h + 1) * HD] * jnp.float32(1.0 / total)


def last_sums(total, *parts):
    vmem = pl.BlockSpec(memory_space=pltpu.VMEM)
    shape = (2, CUT, KO)

    def kernel(*refs):
        last_sums_kernel(total, *refs)

    return pl.pallas_call(
        kernel,
        out_shape=(
            jax.ShapeDtypeStruct(shape, jnp.float32),
            jax.ShapeDtypeStruct(shape, jnp.bfloat16),
            jax.ShapeDtypeStruct((1, KVH, HD, HD), jnp.float32),
        ),
        in_specs=[vmem] * 5,
        out_specs=(vmem,) * 3,
        compiler_params=pltpu.CompilerParams(vmem_limit_bytes=8 * 2**20),
        name="last_sums",
    )(*parts)


def pair_kernel(straight, crossed, head, other, out):
    first = lax.axis_index("dp") & 1

    def turn(top, bottom):
        out[:, :PAIR] = jnp.concatenate([top[:BLK], bottom[:BLK]], axis=0).T

    pl.when(first == 0)(lambda: turn(straight, crossed))
    pl.when(first == 1)(lambda: turn(crossed, straight))
    both = head[...].astype(jnp.float32) + other[...].astype(jnp.float32)
    out[:, PAIR:] = both.astype(jnp.bfloat16)


def weight_pair(straight, crossed, head, other):
    vmem = pl.BlockSpec(memory_space=pltpu.VMEM)
    return pl.pallas_call(
        pair_kernel,
        out_shape=jax.ShapeDtypeStruct((KO, PAIR + HD), jnp.bfloat16),
        in_specs=[vmem] * 4,
        out_specs=vmem,
        compiler_params=pltpu.CompilerParams(vmem_limit_bytes=8 * 2**20),
        name="weight_pair",
    )(straight, crossed, head, other)


def stack_kernel(own, near_a, near_b, near_ab, held_a, held_b, head):
    pieces = (own, near_a, near_b, near_ab)
    for i, piece in enumerate(pieces):
        held_a[i] = piece[: KO // 2, :PAIR]
        held_b[i] = piece[KO // 2 :, :PAIR]
    terms = [piece[:, PAIR:].astype(jnp.float32) for piece in pieces]
    total = ((terms[0] + terms[1]) + (terms[2] + terms[3])).astype(jnp.bfloat16)
    for h in range(KVH):
        head[:, h * HD : (h + 1) * HD] = total[h * HD : (h + 1) * HD]


def stacked(pieces):
    vmem = pl.BlockSpec(memory_space=pltpu.VMEM)
    held = jax.ShapeDtypeStruct((4, KO // 2, PAIR), jnp.bfloat16)
    return pl.pallas_call(
        stack_kernel,
        out_shape=(held, held, jax.ShapeDtypeStruct((HD, KO), jnp.bfloat16)),
        in_specs=[vmem] * 4,
        out_specs=(vmem,) * 3,
        compiler_params=pltpu.CompilerParams(vmem_limit_bytes=8 * 2**20),
        name="stacked",
    )(*pieces)


def finish_kernel(total, slot_ref, keep, got, inv_in, inv_out, precond_ref, gram_ref):
    scale = jnp.float32(1.0 / total)
    sum_a = (keep[0] + got[0].astype(jnp.float32)) * scale
    sum_b = (keep[1] + got[1].astype(jnp.float32)) * scale
    grad = jnp.concatenate([sum_a, sum_b[: BLK - CUT]], axis=0)
    packed = jnp.concatenate(
        [sum_b[BLK - CUT :, c * 128 : (c + 1) * 128] for c in range(4)], axis=0
    )
    odd = slot_ref[0, lax.axis_index("dp")] & 1

    @pl.when(odd == 0)
    def _():
        low = packed[64:]
        turned = low.T
        gram_ref[:64] = jnp.concatenate([packed[:64, :64], turned[:64]], axis=1)
        gram_ref[64:128] = jnp.concatenate([low[:64], turned[64:, 64:]], axis=1)
        gram_ref[128:] = jnp.concatenate([low[64:], packed[:64, 64:]], axis=1)

    @pl.when(odd == 1)
    def _():
        high = packed[:128]
        turned = high.T
        gram_ref[:64] = jnp.concatenate([packed[128:, :64], high[:64]], axis=1)
        gram_ref[64:128] = jnp.concatenate([turned[:64, :64], high[64:]], axis=1)
        gram_ref[128:] = jnp.concatenate([turned[64:], packed[128:, 64:]], axis=1)

    for h in range(KVH):
        cols = slice(h * HD, (h + 1) * HD)
        left = jnp.dot(
            inv_in[0],
            grad[:, cols],
            precision=lax.Precision.HIGHEST,
            preferred_element_type=jnp.float32,
        )
        precond_ref[0, :, cols] = jnp.dot(
            left,
            inv_out[h],
            precision=lax.Precision.HIGHEST,
            preferred_element_type=jnp.float32,
        )


def finished(total, slots, keep, got, inv_in, inv_out):
    vmem = pl.BlockSpec(memory_space=pltpu.VMEM)

    def kernel(*refs):
        finish_kernel(total, *refs)

    return pl.pallas_call(
        kernel,
        out_shape=(
            jax.ShapeDtypeStruct((1, BLK, KO), jnp.float32),
            jax.ShapeDtypeStruct((BLK, BLK), jnp.float32),
        ),
        in_specs=[pl.BlockSpec(memory_space=pltpu.SMEM)] + [vmem] * 4,
        out_specs=(vmem, vmem),
        compiler_params=pltpu.CompilerParams(vmem_limit_bytes=16 * 2**20),
        name="finish",
    )(slots, keep, got, inv_in, inv_out)


def passed_columns(i, ring):
    core, me = my_place()
    rels = [
        sum(bit(i, k) << d for k, d in enumerate(RINGS[c][0]))
        + sum(bit(ring, k) << d for k, d in enumerate(RINGS[c][1]))
        for c in range(2)
    ]
    owner = me ^ jnp.where(core == 0, rels[0], rels[1])
    x, y = gray(owner >> 3), gray((owner >> 1) & 3)
    return pl.ds(pl.multiple_of((x * NY + y) * PAIR, 128), PAIR)


def begin_kernel(held_a, held_b, third_a, third_b, k_ref, resid_ref, out_ref, part):
    keys_a, keys_b = k_ref[BLK:, : KO // 2], k_ref[BLK:, KO // 2 :]
    for i in range(4):
        cols = passed_columns(i, 0)
        branch = dot(keys_a, held_a[i]) + dot(keys_b, held_b[i])
        out_ref[:, cols] = (resid_ref[:, cols].astype(jnp.float32) + branch).astype(jnp.bfloat16)
        part[i] = dot(keys_a, third_a[i])
        part[4 + i] = dot(keys_b, third_b[i])


def passed_begun(*parts):
    vmem = pl.BlockSpec(memory_space=pltpu.VMEM)
    resid = parts[-1]
    return pl.pallas_call(
        begin_kernel,
        out_shape=(
            jax.ShapeDtypeStruct(resid.shape, jnp.bfloat16),
            jax.ShapeDtypeStruct((8, resid.shape[0], PAIR), jnp.float32),
        ),
        in_specs=[vmem] * 6,
        out_specs=(vmem, vmem),
        compiler_params=pltpu.CompilerParams(vmem_limit_bytes=24 * 2**20),
        cost_estimate=pl.CostEstimate(
            flops=256 * 6144 * 512, bytes_accessed=8 * 2**20, transcendentals=0
        ),
        name="passed_begun",
    )(*parts)


def rest_kernel(last_a, last_b, k_ref, resid_ref, part, begun, out_ref, blocks, sems):
    keys_a, keys_b = k_ref[BLK:, : KO // 2], k_ref[BLK:, KO // 2 :]
    copies = []
    for ring in (1, 2, 3):
        for i in range(4):
            if ring == 1:
                branch = part[i] + dot(keys_b, last_b[i])
            elif ring == 2:
                branch = dot(keys_a, last_a[i]) + part[4 + i]
            else:
                branch = dot(keys_a, last_a[4 + i]) + dot(keys_b, last_b[4 + i])
            cols = passed_columns(i, ring)
            at = len(copies)
            total = resid_ref[:, cols].astype(jnp.float32) + branch
            blocks[at] = total.astype(jnp.bfloat16)
            copies.append(pltpu.make_async_copy(blocks.at[at], out_ref.at[:, cols], sems.at[at]))
            copies[at].start()
    for copy in copies:
        copy.wait()


def passed_rest(last_a, last_b, key_pre, resid, part, begun):
    vmem = pl.BlockSpec(memory_space=pltpu.VMEM)
    hbm = pl.BlockSpec(memory_space=pl.ANY)
    return pl.pallas_call(
        rest_kernel,
        out_shape=jax.ShapeDtypeStruct(resid.shape, jnp.bfloat16),
        in_specs=[vmem] * 5 + [hbm],
        out_specs=hbm,
        input_output_aliases={5: 0},
        scratch_shapes=[
            pltpu.VMEM((12, resid.shape[0], PAIR), jnp.bfloat16),
            pltpu.SemaphoreType.DMA((12,)),
        ],
        compiler_params=pltpu.CompilerParams(vmem_limit_bytes=24 * 2**20),
        cost_estimate=pl.CostEstimate(
            flops=256 * 6144 * 512, bytes_accessed=8 * 2**20, transcendentals=0
        ),
        name="passed_rest",
    )(last_a, last_b, key_pre, resid, part, begun)


def hop(block, route):
    return lax.ppermute(block, AXES, route)


def tie(*values):
    return lax.optimization_barrier(values)


def body(
    layer_inputs, resid_grad, key_grad, key_weight, fim_bounds, slot_block, inv_input, inv_head
):
    total = layer_inputs.shape[1] * lax.axis_size("dp")

    key_pre, head, order, weight_and_key = keys_and_order(
        total, slot_block, fim_bounds, key_grad, key_weight
    )
    send_a, send_b, turned = sent_products(order, layer_inputs, key_pre)
    straight = hop(weight_and_key, back_route(False))
    send_a, send_b, head, weight = tie(send_a, send_b, head, key_weight[0])
    first = [hop(x, step_route(SUMS, s, 0)) for s, x in enumerate((send_a, send_b))]
    far_a, far_b, near_a, near_b = kept_products(order, layer_inputs, key_pre, turned)
    crossed = hop(weight, back_route(True))
    other = hop(head, flip_route(((Z,), (Z,))))
    crossed, other, far_a, near_a = tie(crossed, other, far_a, near_a)
    pair = weight_pair(straight, crossed, head, other)
    near = [pair] + [hop(pair, ring_route(0, which)) for which in (1, 2, 3)]
    resid_in, pair = tie(resid_grad[0], pair)
    resid = hop(resid_in, back_route(False))

    far_a, far_b, _ = tie(far_a, far_b, pair)
    sums = halved(far_a, first[0], far_b, first[1])
    second = [hop(sums[s], step_route(SUMS, s, 1)) for s in range(2)]

    held_a, held_b, head = stacked(near)
    held = [held_a, held_b]
    third = [hop(held[s], step_route(WEIGHTS, s, 2)) for s in range(2)]
    second[0], second[1], head = tie(*second, head)
    own, *sent = ring_sums(near_a, first[0], second[0], near_b, first[1], second[1], head)
    ring = [hop(sent[i], ring_route(1, i + 1)) for i in range(3)]
    own, held[0], held[1], third[0], third[1], _, _, _ = tie(own, *held, *third, *ring)
    more = [jnp.concatenate([held[s], third[s]], axis=0) for s in range(2)]
    fourth = [hop(more[s], step_route(WEIGHTS, s, 3)) for s in range(2)]
    keep, send, head_grams = last_sums(total, own, head, *ring)
    last = hop(send, flip_route(((Z,), (Z,))))
    begun, part = passed_begun(*held, *third, straight, resid)
    last, part = tie(last, part)
    passed = passed_rest(*fourth, straight, resid, part, begun)
    precond, gram = finished(total, slot_block, keep, last, inv_input[0], inv_head[0])
    return (passed[None], precond[None], gram[None, None], head_grams)


def solution(mesh):
    return jax.shard_map(
        body,
        mesh=mesh,
        in_specs=(
            P("segment", "dp", None),
            P("segment", "dp", None),
            P("segment", "dp", None),
            P("segment", "dp", None),
            P("segment", None),
            P("segment", None),
            P("segment", "dp", None, None),
            P("segment", None, None, None),
        ),
        out_specs=(
            P("segment", "dp", None),
            P("segment", "dp", None, None),
            P("segment", "dp", None, None),
            P("segment", None, None, None),
        ),
        check_vma=False,
    )
```
